256 devices in a mesh: line: 8 (over x, core), span: 32 (over y, z).
Axes of the slice: x: 4, y: 4, z: 8, core: 2. Of those that a mesh axis runs over, the one named last changes fastest.
Arguments:
- residual: float32 [128, 16, 64, 320], P('span', 'line'), may hold values from -6 to 6
- previous: float32 [128, 16, 64, 320], P('span', 'line'), may hold values from -6 to 6
- pivot_inverse: float32 [128, 16, 320, 320], P('span', 'line')
- lower_blocks: float32 [128, 16, 320, 320], P('span', 'line')
- upper_blocks: float32 [128, 16, 320, 320], P('span', 'line')
- flux_jacobian: float32 [128, 16, 80, 320], P('span', 'line'), may hold values from -0.625 to 0.625
- trace_operator: float32 [320, 320], replicated, may hold values from -0.3125 to 0.3125
- lift_operator: float32 [320, 320], replicated, may hold values from -0.3125 to 0.3125
- lengths: int32 [128], P('span'), may hold values from 8 to 16, as said below
- neighbour_line: int32 [128, 4], P('span'), may hold values from 0 to 127, as said below
- neighbour_face: int32 [128, 4], P('span'), may hold values from 0 to 3
Outputs:
- update: float32 [128, 16, 64, 320], P('span', 'line')
The draws below stay inside these ranges and needn't reach their ends.
Inputs may be any that keep to these rules, and one draw needn't show every extreme that they name: `lengths`: every line has between 8 and 16 elements; some line has 16 and some line 16 // 2. `neighbour_line`: no line is its own neighbour; neighbours may lie anywhere in the span numbering.
All inputs are finite; a program needn't handle non-finite values.
Results may differ from the reference program's by a relative error of at most 0.0001.
Values sent between devices are 32-bit elements; how exact they have to be, the bound alone decides.
No kernel may reach another device: no remote copies, remote signals or barrier semaphores. Data moves between devices by JAX's collectives and lax.ppermute only.
A program may use at most 192 MiB of HBM per device.

```python
import math
import jax
import jax.numpy as jnp
from jax import lax

NB = 320
NF = 80
FACES = 4
NV = 64
LINES = 128
NE = 16


def block_draw(key, diag_values, sigma):
    shape = diag_values.shape + (NB,)
    spread = sigma * jnp.clip(jax.random.normal(key, shape, jnp.float32), -3.0, 3.0)
    identity_mat = jnp.eye(NB, dtype=jnp.float32)
    return identity_mat * diag_values[..., None] + (1.0 - identity_mat) * spread


def transfer_draw(key):
    key_kind, key_slow, key_fast, key_off = jax.random.split(key, 4)
    shape = (LINES, NE, NB)
    slow_share = 0.5
    slow_flag = jax.random.bernoulli(key_kind, slow_share, shape)
    slow_rate = jax.random.uniform(key_slow, shape, jnp.float32, 0.9, 0.97)
    fast_rate = jax.random.uniform(key_fast, shape, jnp.float32, 0.2, 0.6)
    return block_draw(key_off, jnp.where(slow_flag, slow_rate, fast_rate), 0.01)


def draw_pivot_inverse(key, part):
    key_diag, key_off = jax.random.split(jax.random.fold_in(key, 5))
    diag_values = jnp.exp(jax.random.uniform(key_diag, (LINES, NE, NB), jnp.float32, math.log(0.15), math.log(0.6)))
    return block_draw(key_off, diag_values, 0.02)


def draw_lower_blocks(key, part):
    return transfer_draw(jax.random.fold_in(key, 11))


def draw_upper_blocks(key, part):
    return transfer_draw(jax.random.fold_in(key, 23))


def draw_lengths(key, part):
    key_base, key_first, key_second = jax.random.split(jax.random.fold_in(key, 31), 3)
    shortest = NE // 2
    drawn = jax.random.randint(key_base, (LINES,), shortest, NE + 1, dtype=jnp.int32)
    longest_line = jax.random.randint(key_first, (), 0, LINES, dtype=jnp.int32)
    shortest_line = (longest_line + 1 + jax.random.randint(key_second, (), 0, LINES - 1, dtype=jnp.int32)) % LINES
    drawn = drawn.at[longest_line].set(NE)
    drawn = drawn.at[shortest_line].set(shortest)
    return drawn


def draw_neighbour_line(key, part):
    offsets = jax.random.randint(jax.random.fold_in(key, 47), (LINES, FACES), 1, LINES, dtype=jnp.int32)
    offsets = offsets.at[0, 0].set(LINES - 1)
    offsets = offsets.at[1, 0].set(LINES - 1)
    line_ids = jnp.arange(LINES, dtype=jnp.int32)[:, None]
    return (line_ids + offsets) % LINES


def place_ends(array, rng, smallest, high):
    longest = array.shape.index(max(array.shape))
    spots = []
    for shift in (0, 1):
        where = [jax.random.randint(jax.random.fold_in(rng, axis), (), 0, length) for axis, length in enumerate(array.shape)]
        where[longest] = (where[longest] + shift) % array.shape[longest]
        spots.append(tuple(where))
    return array.at[spots[0]].set(smallest).at[spots[1]].set(high)


def steps_of(rng, dims, cuts, smallest, top_value):
    def one(dim, parts):
        draws = jax.random.uniform(jax.random.fold_in(jax.random.fold_in(rng, 6), dim), (parts,), jnp.float32, smallest / len(cuts), top_value / len(cuts))
        return jnp.repeat(jnp.exp(draws), dims[dim] // parts).reshape((-1,) + (1,) * (len(dims) - dim - 1))

    factor_of = one(*cuts[0])
    for cut in cuts[1:]:
        factor_of = factor_of * one(*cut)
    return factor_of


def scatter_about(own_key, shape, scale, most, shards=(), held_as=jnp.bfloat16):
    entries = scale * jax.random.normal(own_key, shape, jnp.float32)
    if shards:
        entries = entries * steps_of(own_key, shape, shards, -0.22, 0.18)
    return jnp.clip(entries, -most, most).astype(held_as)


def setup_inputs(seed: int = 0) -> dict:
    keys = jax.random.split(jax.random.key(seed), 12)
    residual = scatter_about(keys[0], (LINES, NE, NV, NB), 1.0, 6.0, ((0, 32), (1, 8)), jnp.float32)
    previous = scatter_about(keys[1], (LINES, NE, NV, NB), 1.0, 6.0, ((0, 32), (1, 8)), jnp.float32)
    pivot_inverse = draw_pivot_inverse(jax.random.fold_in(keys[11], 71), 0)
    lower_blocks = draw_lower_blocks(jax.random.fold_in(keys[11], 71), 0)
    upper_blocks = draw_upper_blocks(jax.random.fold_in(keys[11], 71), 0)
    flux_jacobian = scatter_about(keys[5], (LINES, NE, NF, FACES * NF), NF ** -0.5, 0.625, ((0, 32), (1, 8)), jnp.float32)
    trace_operator = scatter_about(keys[6], (NB, FACES * NF), NB ** -0.5, 0.3125, (), jnp.float32)
    lift_operator = scatter_about(keys[7], (FACES * NF, NB), (FACES * NF) ** -0.5, 0.3125, (), jnp.float32)
    lengths = draw_lengths(jax.random.fold_in(keys[11], 71), 0)
    neighbour_line = draw_neighbour_line(jax.random.fold_in(keys[11], 71), 0)
    neighbour_face = place_ends(jax.random.randint(keys[10], (LINES, FACES), 0, FACES), jax.random.fold_in(keys[10], 1), 0, FACES - 1).astype(jnp.int32)
    return dict(residual=residual, previous=previous, pivot_inverse=pivot_inverse, lower_blocks=lower_blocks, upper_blocks=upper_blocks, flux_jacobian=flux_jacobian, trace_operator=trace_operator, lift_operator=lift_operator, lengths=lengths, neighbour_line=neighbour_line, neighbour_face=neighbour_face)


def reference(residual, previous, pivot_inverse, lower_blocks, upper_blocks, flux_jacobian, trace_operator, lift_operator, lengths, neighbour_line, neighbour_face):
    highest = lax.Precision.HIGHEST
    position = jnp.arange(NE, dtype=jnp.int32)
    live = (position[None, :] < lengths[:, None]).astype(jnp.float32)
    masked = previous * live[:, :, None, None]
    traces = jnp.einsum("levn,nk->levk", masked, trace_operator, precision=highest)
    face_index = jnp.arange(FACES, dtype=jnp.int32)
    gathered = []
    for face_slot in range(FACES):
        remote = traces[neighbour_line[:, face_slot]].reshape(LINES, NE, NV, FACES, NF)
        select = (neighbour_face[:, face_slot, None] == face_index[None, :]).astype(jnp.float32)
        gathered.append(jnp.einsum("levgk,lg->levk", remote, select, precision=highest))
    neighbour_trace = jnp.stack(gathered, axis=3)
    jacobian = flux_jacobian.reshape(LINES, NE, NF, FACES, NF)
    face_flux = jnp.einsum("leifj,levfj->levfi", jacobian, neighbour_trace, precision=highest)
    face_term = jnp.einsum("levm,mn->levn", face_flux.reshape(LINES, NE, NV, FACES * NF), lift_operator, precision=highest)
    driving = jnp.einsum("leij,levj->levi", pivot_inverse, residual, precision=highest) - jnp.einsum("leij,levj->levi", pivot_inverse, face_term, precision=highest)
    carried = jnp.zeros((LINES, NV, NB), jnp.float32)
    sweep_list = []
    for element in range(NE):
        carried = live[:, element, None, None] * (driving[:, element] + jnp.einsum("lij,lvj->lvi", lower_blocks[:, element], carried, precision=highest))
        sweep_list.append(carried)
    carried = jnp.zeros((LINES, NV, NB), jnp.float32)
    update_list = [None] * NE
    for element in reversed(range(NE)):
        carried = live[:, element, None, None] * (sweep_list[element] + jnp.einsum("lij,lvj->lvi", upper_blocks[:, element], carried, precision=highest))
        update_list[element] = carried
    return jnp.stack(update_list, axis=1)
```

```python
import jax
import jax.numpy as jnp
from jax import lax
from jax.experimental import pallas as pl
from jax.experimental.pallas import tpu as pltpu
from jax.sharding import PartitionSpec as P

NB = 320
NF = 80
FACES = 4
NV = 64
ROW = 128
YS, ZS = 4, 8
LINE_ROWS = 4
SLOTS = LINE_ROWS * FACES
HALF = SLOTS // 2


VMEM = pl.BlockSpec(memory_space=pltpu.VMEM)
SMEM = pl.BlockSpec(memory_space=pltpu.SMEM)


def f32(*shape):
    return jax.ShapeDtypeStruct(shape, jnp.float32)


def z_shift(array, by):
    pairs = [(y * ZS + z, y * ZS + (z + by) % ZS) for y in range(YS) for z in range(ZS)]
    return lax.ppermute(array, "span", pairs)


def y_shift(array, by):
    pairs = [(y * ZS + z, (y + by) % YS * ZS + z) for y in range(YS) for z in range(ZS)]
    return lax.ppermute(array, "span", pairs)


def core_swap(array):
    return lax.ppermute(array, "line", [(i, i ^ 1) for i in range(8)])


def chip_shift(array, by, chips=range(4)):
    pairs = [
        (2 * x + core, 2 * (x + by) + core)
        for x in chips
        for core in range(2)
        if 0 <= x + by < 4
    ]
    return lax.ppermute(array, "line", pairs)


def high_low(array):
    high = lax.reduce_precision(array, 8, 7)
    return high.astype(jnp.bfloat16), (array - high).astype(jnp.bfloat16)


def split_value(x):
    high = x.astype(jnp.bfloat16)
    return high, (x - high.astype(jnp.float32)).astype(jnp.bfloat16)


def product(w_high, w_low, x_high, x_both):
    wide = jnp.dot(w_high, x_both, preferred_element_type=jnp.float32)
    low = jnp.dot(w_low, x_high, preferred_element_type=jnp.float32)
    return wide[:, :ROW] + wide[:, ROW:] + low


def left_lanes():
    return lax.broadcasted_iota(jnp.int32, (NB, ROW), 1) < NV


def apply_pair(w_high, w_low, first, second, x):
    high, low = split_value(x)
    both = jnp.concatenate([high, low], axis=1)
    left = product(w_high[first], w_low[first], high, both)
    right = product(w_high[second], w_low[second], high, both)
    return jnp.where(left_lanes(), left, right)


def pick_kernel(table, place, own, up1, up2, up3, down1, down2, down3, up4, down4,
                mine, next_a, next_b, prev_a, prev_b, far_a, far_b):
    y, z = place[0], place[1]
    whole = ((0, own), (7, up1), (6, up2), (5, up3), (1, down1), (2, down2), (3, down3))

    def fill(dy, first, count, out, out_first):
        def body(i, carry):
            asked = table[dy, first + i]
            owner, piece = asked // SLOTS, asked % SLOTS
            dz = (owner % ZS - z + ZS) % ZS

            @pl.when(owner // ZS == y)
            def _():
                for k, source in whole:
                    @pl.when(dz == k)
                    def _():
                        out[out_first + i] = source[piece]

                @pl.when((dz == 4) & (piece < HALF))
                def _():
                    out[out_first + i] = up4[jnp.minimum(piece, HALF - 1)]

                @pl.when((dz == 4) & (piece >= HALF))
                def _():
                    out[out_first + i] = down4[jnp.maximum(piece - HALF, 0)]

            return carry

        lax.fori_loop(0, count, body, 0)

    fill(2, 0, HALF, far_a, 0)
    fill(2, HALF, HALF, far_b, 0)
    fill(1, 0, HALF, next_a, 0)
    fill(1, HALF, HALF, next_b, 0)
    fill(3, 0, HALF, prev_a, 0)
    fill(3, HALF, HALF, prev_b, 0)
    fill(0, 0, SLOTS, mine, 0)


def merge_kernel(table, place, next_a, prev_b, far_a, far_b, out_next, out_prev):
    y = place[0]

    def body(i, carry):
        up = table[1, i] // (SLOTS * ZS)
        out_next[i] = jnp.where(up == (y + YS - 1) % YS, far_a[i], next_a[i])
        down = table[3, HALF + i] // (SLOTS * ZS)
        out_prev[i] = jnp.where(down == (y + 1) % YS, far_b[i], prev_b[i])
        return carry

    lax.fori_loop(0, HALF, body, 0)


def driving_kernel(table, place, live, mine, below_a, below_b, above_a, above_b,
                   w_high, w_low, own, out, held):
    y = place[0]
    left = left_lanes()
    for pair in range(2):
        below, above = ((below_a, above_a), (below_b, above_b))[pair]
        lines = []
        for row in range(2):
            line = 2 * pair + row
            for face in range(FACES):
                slot = line * FACES + face
                place_in = slot - pair * HALF
                dy = (table[0, slot] // (SLOTS * ZS) - y + YS) % YS
                from_below = (dy == 3) | ((dy == 2) & (pair == 0))
                value = jnp.where(from_below, below[place_in], above[place_in])
                value = jnp.where(dy == 0, mine[slot], value)
                held[pl.ds(face * NF, NF), :] = value
            term = apply_pair(w_high, w_low, 2 * line, 2 * line + 1, held[...])
            lines.append(own[line] - term)
        first, second = lines
        for element in range(2):
            if element == 0:
                both = jnp.where(left, first, pltpu.roll(second, NV, 1))
            else:
                both = jnp.where(left, pltpu.roll(first, NV, 1), second)
            alive = jnp.where(left, live[2 * pair, element], live[2 * pair + 1, element])
            out[pair, element] = both * alive


def forward_kernel(core, kept, came, l_high, l_low, out, last):
    first = core[0] == 0
    value = None
    for element in range(4):
        pair = (kept, came) if element < 2 else (came, kept)
        term = jnp.where(first, pair[0][element % 2], pair[1][element % 2])
        out[element] = term
        if element:
            term = term + apply_pair(l_high, l_low, element, 4 + element, value)
        value = term
    last[...] = value


def middle_kernel(near, mid, far, m1_high, m1_low, m2_high, m2_low, driving,
                  l_high, l_low, u_high, u_low, sweep, first):
    value = mid[...] + apply_pair(m2_high, m2_low, 0, 1, far[...])
    value = near[...] + apply_pair(m1_high, m1_low, 0, 1, value)
    for element in range(4):
        value = driving[element] + apply_pair(l_high, l_low, element, 4 + element, value)
        sweep[element] = value
    for element in (2, 1, 0):
        value = sweep[element] + apply_pair(u_high, u_low, element, 4 + element, value)
    first[...] = value


def backward_kernel(core, near, mid, far, n1_high, n1_low, n2_high, n2_low, sweep,
                    u_high, u_low, out):
    value = mid[...] + apply_pair(n2_high, n2_low, 0, 1, far[...])
    value = near[...] + apply_pair(n1_high, n1_low, 0, 1, value)
    for element in (3, 2, 1, 0):
        value = sweep[element] + apply_pair(u_high, u_low, element, 4 + element, value)
        natural = jnp.transpose(value)
        half = (element // 2 + core[0]) % 2
        out[half, 0, element % 2] = natural[:NV]
        out[half, 1, element % 2] = natural[NV:]


def call(kernel, name, specs, out_shape, operands, flops, scratch=()):
    out_specs = jax.tree.map(lambda _: VMEM, out_shape)
    moved = sum(4 * o.size for o in operands) + sum(4 * o.size for o in jax.tree.leaves(out_shape))
    return pl.pallas_call(
        kernel,
        name=name,
        out_shape=out_shape,
        in_specs=specs,
        out_specs=out_specs,
        scratch_shapes=list(scratch),
        cost_estimate=pl.CostEstimate(flops=flops, bytes_accessed=moved, transcendentals=0),
    )(*operands)


def local(
    residual,
    previous,
    pivot_inverse,
    lower_blocks,
    upper_blocks,
    flux_jacobian,
    trace_operator,
    lift_operator,
    lengths,
    neighbour_line,
    neighbour_face,
):
    high = lax.Precision.HIGH
    line_pos = lax.axis_index("line")
    span_pos = lax.axis_index("span")
    core = line_pos % 2
    elements = residual.shape[1]
    position = line_pos * elements + jnp.arange(elements, dtype=jnp.int32)
    live = (position[None, :] < lengths[:, None]).astype(jnp.float32)
    place = jnp.stack([span_pos // ZS, span_pos % ZS]).astype(jnp.int32)
    core_ref = core.astype(jnp.int32).reshape(1)

    masked = (previous * live[:, :, None, None]).reshape(LINE_ROWS, ROW, NB)
    own = jnp.einsum("lmn,nk->lkm", masked, trace_operator, precision=high)
    own = own.reshape(SLOTS, NF, ROW)

    asked = (neighbour_line * FACES + neighbour_face).reshape(SLOTS)
    table = jnp.stack([asked, y_shift(asked, -1), y_shift(asked, 2), y_shift(asked, 1)])

    up1 = z_shift(own, 1)
    down1 = z_shift(own, -1)
    up2 = z_shift(up1, 1)
    down2 = z_shift(down1, -1)
    up3 = z_shift(up2, 1)
    down3 = z_shift(down2, -1)
    up4 = z_shift(up3[:HALF], 1)
    down4 = z_shift(down3[HALF:], -1)

    def both_lines(blocks):
        blocks = blocks * live[:, :, None, None]
        kept = lax.dynamic_slice_in_dim(blocks, core * 2, 2, 0)
        came = core_swap(lax.dynamic_slice_in_dim(blocks, (1 - core) * 2, 2, 0))
        return jnp.where(
            core == 0,
            jnp.concatenate([kept, came], axis=1),
            jnp.concatenate([came, kept], axis=1),
        )

    def chain(blocks):
        total = blocks[0]
        for block in blocks[1:]:
            total = jnp.einsum("lij,ljk->lik", total, block, precision=high)
        return total

    lower = both_lines(lower_blocks)
    upper = both_lines(upper_blocks)
    up_all = chain([lower[:, e] for e in (3, 2, 1, 0)])
    down_all = chain([upper[:, e] for e in (0, 1, 2, 3)])
    m1 = high_low(chip_shift(up_all, 1, (1, 2)))
    m2 = high_low(chip_shift(up_all, 2, (1,)))
    n1 = high_low(chip_shift(down_all, -1, (2, 1)))
    n2 = high_low(chip_shift(down_all, -2, (2,)))
    l_split = [part.reshape(8, NB, NB) for part in high_low(lower)]
    u_split = [part.reshape(8, NB, NB) for part in high_low(upper)]

    faces = jnp.arange(NB) // NF
    tiled = jnp.tile(flux_jacobian, (1, 1, FACES, 1))
    tiled = jnp.where(faces[:, None] == faces[None, :], tiled, 0.0)
    lifted = jnp.einsum("mn,lemk->lenk", lift_operator, tiled, precision=high)
    face_map = jnp.einsum("lein,lenk->leik", pivot_inverse, lifted, precision=high)
    k_split = [part.reshape(8, NB, NB) for part in high_low(face_map)]
    driving_own = jnp.einsum("leij,levj->liev", pivot_inverse, residual, precision=high)
    driving_own = driving_own.reshape(LINE_ROWS, NB, ROW)

    mine, next_a, next_b, prev_a, prev_b, far_a, far_b = call(
        pick_kernel, "pick", [SMEM] * 2 + [VMEM] * 9,
        [f32(SLOTS, NF, ROW)] + [f32(HALF, NF, ROW)] * 6,
        (table, place, own, up1, up2, up3, down1, down2, down3, up4, down4), 0,
    )
    far_a = y_shift(far_a, 1)
    far_b = y_shift(far_b, -1)
    below_b = y_shift(next_b, 1)
    above_a = y_shift(prev_a, -1)
    next_a, prev_b = call(
        merge_kernel, "merge", [SMEM] * 2 + [VMEM] * 4, [f32(HALF, NF, ROW)] * 2,
        (table, place, next_a, prev_b, far_a, far_b), 0,
    )
    below_a = y_shift(next_a, 1)
    above_b = y_shift(prev_b, -1)

    matmul = 2 * NB * NB * ROW * 3
    driving = call(
        driving_kernel, "driving", [SMEM] * 3 + [VMEM] * 8, f32(2, 2, NB, ROW),
        (table, place, live, mine, below_a, below_b, above_a, above_b, *k_split, driving_own),
        8 * matmul, [pltpu.VMEM((NB, ROW), jnp.float32)],
    )
    kept = lax.dynamic_index_in_dim(driving, core, 0, keepdims=False)
    came = core_swap(lax.dynamic_index_in_dim(driving, 1 - core, 0, keepdims=False))
    driving, last = call(
        forward_kernel, "forward", [SMEM] + [VMEM] * 4, [f32(4, NB, ROW), f32(NB, ROW)],
        (core_ref, kept, came, *l_split), 6 * matmul,
    )
    sweep, first = call(
        middle_kernel, "middle", [VMEM] * 12, [f32(4, NB, ROW), f32(NB, ROW)],
        (chip_shift(last, 1), chip_shift(last, 2), chip_shift(last, 3),
         *m1, *m2, driving, *l_split, *u_split), 18 * matmul,
    )
    halves = call(
        backward_kernel, "backward", [SMEM] + [VMEM] * 10, f32(2, 2, 2, NV, NB),
        (core_ref, chip_shift(first, -1), chip_shift(first, -2), chip_shift(first, -3),
         *n1, *n2, sweep, *u_split), 12 * matmul,
    )
    came = core_swap(halves[1])
    return jnp.where(
        core == 0,
        jnp.concatenate([halves[0], came], axis=0),
        jnp.concatenate([came, halves[0]], axis=0),
    )


def solution(mesh):
    return jax.shard_map(
        local,
        mesh=mesh,
        in_specs=(
            P("span", "line", None, None),
            P("span", "line", None, None),
            P("span", "line", None, None),
            P("span", "line", None, None),
            P("span", "line", None, None),
            P("span", "line", None, None),
            P(),
            P(),
            P("span"),
            P("span", None),
            P("span", None),
        ),
        out_specs=P("span", "line", None, None),
        check_vma=False,
    )
```

```python
import jax
import jax.numpy as jnp
from jax import lax
from jax.experimental import pallas as pl
from jax.experimental.pallas import tpu as pltpu
from jax.sharding import PartitionSpec as P

NB = 320
NF = 80
FACES = 4
NV = 64
ROW = 128
YS, ZS = 4, 8
LINE_ROWS = 4
SLOTS = LINE_ROWS * FACES
HALF = SLOTS // 2


VMEM = pl.BlockSpec(memory_space=pltpu.VMEM)
SMEM = pl.BlockSpec(memory_space=pltpu.SMEM)


def f32(*shape):
    return jax.ShapeDtypeStruct(shape, jnp.float32)


def z_shift(array, by):
    pairs = [(y * ZS + z, y * ZS + (z + by) % ZS) for y in range(YS) for z in range(ZS)]
    return lax.ppermute(array, "span", pairs)


def y_shift(array, by):
    pairs = [(y * ZS + z, (y + by) % YS * ZS + z) for y in range(YS) for z in range(ZS)]
    return lax.ppermute(array, "span", pairs)


def core_swap(array):
    return lax.ppermute(array, "line", [(i, i ^ 1) for i in range(8)])


def chip_shift(array, by, chips=range(4)):
    pairs = [
        (2 * x + core, 2 * (x + by) + core)
        for x in chips
        for core in range(2)
        if 0 <= x + by < 4
    ]
    return lax.ppermute(array, "line", pairs)


def high_low(array):
    high = lax.reduce_precision(array, 8, 7)
    return high.astype(jnp.bfloat16), (array - high).astype(jnp.bfloat16)


def split_value(x):
    high = x.astype(jnp.bfloat16)
    return high, (x - high.astype(jnp.float32)).astype(jnp.bfloat16)


def product(w_high, w_low, x_high, x_both):
    wide = jnp.dot(w_high, x_both, preferred_element_type=jnp.float32)
    low = jnp.dot(w_low, x_high, preferred_element_type=jnp.float32)
    return wide[:, :ROW] + wide[:, ROW:] + low


def left_lanes():
    return lax.broadcasted_iota(jnp.int32, (NB, ROW), 1) < NV


def apply_pair(w_high, w_low, first, second, x):
    high, low = split_value(x)
    both = jnp.concatenate([high, low], axis=1)
    left = product(w_high[first], w_low[first], high, both)
    right = product(w_high[second], w_low[second], high, both)
    return jnp.where(left_lanes(), left, right)


def pick_kernel(parts, merges):
    def kernel(table, place, own, up1, up2, up3, down1, down2, down3, up4, down4, *refs):
        y, z = place[0], place[1]
        whole = ((0, own), (7, up1), (6, up2), (5, up3), (1, down1), (2, down2), (3, down3))
        relays, outs = refs[: len(merges)], refs[len(merges) :]
        for number, (out, (dy, first, count)) in enumerate(zip(outs, parts)):

            def body(i, carry):
                asked = table[dy, first + i]
                owner, piece = asked // SLOTS, asked % SLOTS
                dz = (owner % ZS - z + ZS) % ZS

                @pl.when(owner // ZS == y)
                def _():
                    for k, source in whole:
                        @pl.when(dz == k)
                        def _():
                            out[i] = source[piece]

                    @pl.when((dz == 4) & (piece < HALF))
                    def _():
                        out[i] = up4[jnp.minimum(piece, HALF - 1)]

                    @pl.when((dz == 4) & (piece >= HALF))
                    def _():
                        out[i] = down4[jnp.maximum(piece - HALF, 0)]

                if merges:
                    @pl.when(owner // ZS == (y + merges[number]) % YS)
                    def _():
                        out[i] = relays[number][i]

                return carry

            lax.fori_loop(0, count, body, 0)

    return kernel


def halves_kernel(up, down, up_half, down_half):
    up_half[...] = up[:HALF]
    down_half[...] = down[HALF:]


def whole_product(left, right_high, right_low):
    high, low = split_value(left)
    total = jnp.dot(high, right_high, preferred_element_type=jnp.float32)
    total += jnp.dot(low, right_high, preferred_element_type=jnp.float32)
    return total + jnp.dot(high, right_low, preferred_element_type=jnp.float32)


def own_kernel(pivot, residual, high, low, own):
    halves = []
    across = (((1,), (1,)), ((), ()))
    for element in range(2):
        high[0, element], low[0, element] = split_value(pivot[0, element])
        given_high, given_low = split_value(residual[0, element])
        value = lax.dot_general(
            high[0, element], given_high, across, preferred_element_type=jnp.float32
        )
        value += lax.dot_general(
            high[0, element], given_low, across, preferred_element_type=jnp.float32
        )
        value += lax.dot_general(
            low[0, element], given_high, across, preferred_element_type=jnp.float32
        )
        halves.append(value)
    own[0] = jnp.concatenate(halves, axis=1)


def chain_kernel(order):
    def kernel(core, alive, kept, came, high, low, total):
        first = core[0] == 0
        for element in range(4):
            pair = (kept, came) if element < 2 else (came, kept)
            block = jnp.where(first, pair[0][0, element % 2], pair[1][0, element % 2])
            high[0, element], low[0, element] = split_value(block)
            if element == order[0]:
                start = block
        value = start
        for element in order[1:]:
            value = whole_product(value, high[0, element], low[0, element])
        total[0] = value * alive[pl.program_id(0), 3]

    return kernel


def driving_kernel(table, place, core, mine, below_a, below_b, above_a, above_b,
                   jacobian, lift_high, lift_low, pivot_high, pivot_low, own,
                   kept, sent, held, lines):
    y = place[0]
    left = left_lanes()
    row = lax.broadcasted_iota(jnp.int32, (NB, NB), 0) // NF
    column = lax.broadcasted_iota(jnp.int32, (NB, NB), 1) // NF
    own_face = row == column

    def line_step(line, carry):
        for face in range(FACES):
            slot = line * FACES + face
            place_in = slot % HALF
            dy = (table[0, slot] // (SLOTS * ZS) - y + YS) % YS
            lower_half = line < LINE_ROWS // 2
            below = jnp.where(lower_half, below_a[place_in], below_b[place_in])
            above = jnp.where(lower_half, above_a[place_in], above_b[place_in])
            value = jnp.where((dy == 3) | ((dy == 2) & lower_half), below, above)
            held[pl.ds(face * NF, NF), :] = jnp.where(dy == 0, mine[slot], value)
        high, low = split_value(held[...])
        both = jnp.concatenate([high, low], axis=1)
        fluxes = []
        for element in range(2):
            tiled = jnp.concatenate([jacobian[line, element]] * FACES, axis=0)
            wide = split_value(jnp.where(own_face, tiled, 0.0))
            fluxes.append(product(*wide, high, both))
        high, low = split_value(jnp.where(left, *fluxes))
        both = jnp.concatenate([high, low], axis=1)
        term = product(lift_high[...], lift_low[...], high, both)
        lines[line] = own[line] - apply_pair(pivot_high.at[line], pivot_low.at[line], 0, 1, term)
        return carry

    lax.fori_loop(0, LINE_ROWS, line_step, 0)
    for pair in range(2):
        first, second = lines[2 * pair], lines[2 * pair + 1]
        values = (
            jnp.where(left, first, pltpu.roll(second, NV, 1)),
            jnp.where(left, pltpu.roll(first, NV, 1), second),
        )

        @pl.when(core[0] == pair)
        def _():
            kept[0], kept[1] = values

        @pl.when(core[0] != pair)
        def _():
            sent[0], sent[1] = values


def alive_lanes(alive, element):
    lane = lax.broadcasted_iota(jnp.int32, (1, ROW), 1)
    return jnp.where(lane < NV, alive[0, element], alive[1, element])


def forward_kernel(core, alive, kept, came, l_high, l_low, out, last):
    first = core[0] == 0
    for element in range(4):
        pair = (kept, came) if element < 2 else (came, kept)
        out[element] = jnp.where(first, pair[0][element % 2], pair[1][element % 2])
    last[...] = out[0] * alive_lanes(alive, 0)

    def step(element, carry):
        term = apply_pair(l_high, l_low, element, 4 + element, last[...])
        last[...] = (out[element] + term) * alive_lanes(alive, element)
        return carry

    lax.fori_loop(1, 4, step, 0)


def enter(near, mid, far, close, apart):
    value = mid[...] + apply_pair(*apart, 0, 1, far[...])
    return near[...] + apply_pair(*close, 0, 1, value)


def split_blocks(source, high, low):
    for line in range(2):
        high[line], low[line] = split_value(source[line])


def middle_kernel(alive, near, mid, far, close, apart, driving,
                  l_high, l_low, u_high, u_low, sweep, first, *split):
    split_blocks(close, *split[:2])
    split_blocks(apart, *split[2:])
    first[...] = enter(near, mid, far, split[:2], split[2:])

    def up(element, carry):
        term = apply_pair(l_high, l_low, element, 4 + element, first[...])
        first[...] = (driving[element] + term) * alive_lanes(alive, element)
        sweep[element] = first[...]
        return carry

    lax.fori_loop(0, 4, up, 0)

    def down(step, carry):
        element = 2 - step
        term = apply_pair(u_high, u_low, element, 4 + element, first[...])
        first[...] = (sweep[element] + term) * alive_lanes(alive, element)
        return carry

    lax.fori_loop(0, 3, down, 0)


def backward_kernel(core, alive, near, mid, far, close, apart, sweep,
                    u_high, u_low, kept, sent, held, *split):
    split_blocks(close, *split[:2])
    split_blocks(apart, *split[2:])
    held[...] = enter(near, mid, far, split[:2], split[2:])

    def down(step, carry):
        element = 3 - step
        term = apply_pair(u_high, u_low, element, 4 + element, held[...])
        value = (sweep[element] + term) * alive_lanes(alive, element)
        held[...] = value
        natural = jnp.transpose(value)

        @pl.when(element // 2 == core[0])
        def _():
            kept[0, element % 2] = natural[:NV]
            kept[1, element % 2] = natural[NV:]

        @pl.when(element // 2 != core[0])
        def _():
            sent[0, element % 2] = natural[:NV]
            sent[1, element % 2] = natural[NV:]

        return carry

    lax.fori_loop(0, 4, down, 0)


def call(kernel, name, specs, out_shape, operands, flops, scratch=(), mib=16):
    out_specs = jax.tree.map(lambda _: VMEM, out_shape)
    moved = sum(4 * o.size for o in jax.tree.leaves((operands, out_shape)))
    return pl.pallas_call(
        kernel,
        name=name,
        out_shape=out_shape,
        in_specs=specs,
        out_specs=out_specs,
        scratch_shapes=list(scratch),
        compiler_params=pltpu.CompilerParams(vmem_limit_bytes=mib << 20),
        cost_estimate=pl.CostEstimate(flops=flops, bytes_accessed=moved, transcendentals=0),
    )(*operands)


def local(
    residual,
    previous,
    pivot_inverse,
    lower_blocks,
    upper_blocks,
    flux_jacobian,
    trace_operator,
    lift_operator,
    lengths,
    neighbour_line,
    neighbour_face,
):
    high = lax.Precision.HIGH
    line_pos = lax.axis_index("line")
    span_pos = lax.axis_index("span")
    core = line_pos % 2
    elements = residual.shape[1]
    position = line_pos * elements + jnp.arange(elements, dtype=jnp.int32)
    live = (position[None, :] < lengths[:, None]).astype(jnp.float32)
    place = jnp.stack([span_pos // ZS, span_pos % ZS]).astype(jnp.int32)
    core_ref = core.astype(jnp.int32).reshape(1)

    masked = (previous * live[:, :, None, None]).reshape(LINE_ROWS, ROW, NB)
    own = jnp.einsum("lmn,nk->lkm", masked, trace_operator, precision=high)
    own = own.reshape(SLOTS, NF, ROW)

    chip_position = line_pos // 2 * 4 + jnp.arange(4, dtype=jnp.int32)
    chip_lengths = lax.dynamic_slice_in_dim(lengths, core * 2, 2, 0)
    alive = (chip_position[None, :] < chip_lengths[:, None]).astype(jnp.float32)
    block = (1, 2, NB, NB)

    def came_blocks(blocks):
        return core_swap(blocks)

    def chip_chain(blocks, came, order):
        split_shape = jax.ShapeDtypeStruct((2, 4, NB, NB), jnp.bfloat16)
        split_spec = pl.BlockSpec((1, 4, NB, NB), lambda i, core, alive: (i, 0, 0, 0))
        split_high, split_low, total = pl.pallas_call(
            chain_kernel(order),
            name="chain",
            grid_spec=pltpu.PrefetchScalarGridSpec(
                num_scalar_prefetch=2,
                grid=(2,),
                in_specs=[
                    pl.BlockSpec(block, lambda i, core, alive: (core[0] * 2 + i, 0, 0, 0)),
                    pl.BlockSpec(block, lambda i, core, alive: (core[0] * 2 + i, 0, 0, 0)),
                ],
                out_specs=[
                    split_spec,
                    split_spec,
                    pl.BlockSpec((1, NB, NB), lambda i, core, alive: (i, 0, 0)),
                ],
            ),
            out_shape=[split_shape, split_shape, f32(2, NB, NB)],
            compiler_params=pltpu.CompilerParams(vmem_limit_bytes=60 << 20),
            cost_estimate=pl.CostEstimate(
                flops=36 * NB**3, bytes_accessed=32 * NB * NB, transcendentals=0
            ),
        )(core_ref, alive, blocks, came)
        return (split_high.reshape(8, NB, NB), split_low.reshape(8, NB, NB)), total

    def pivot_parts():
        split_shape = jax.ShapeDtypeStruct((LINE_ROWS, 2, NB, NB), jnp.bfloat16)
        spec = pl.BlockSpec(block, lambda i: (i, 0, 0, 0))
        return pl.pallas_call(
            own_kernel,
            name="own",
            grid=(LINE_ROWS,),
            in_specs=[spec, pl.BlockSpec((1, 2, NV, NB), lambda i: (i, 0, 0, 0))],
            out_specs=[spec, spec, pl.BlockSpec((1, NB, ROW), lambda i: (i, 0, 0))],
            out_shape=[split_shape, split_shape, f32(LINE_ROWS, NB, ROW)],
            compiler_params=pltpu.CompilerParams(vmem_limit_bytes=60 << 20),
            cost_estimate=pl.CostEstimate(
                flops=48 * NB * NB * NV, bytes_accessed=64 * NB * NB, transcendentals=0
            ),
        )(pivot_inverse, residual)

    (own, residual, pivot_inverse, lower_blocks, upper_blocks, flux_jacobian, lift_operator,
     neighbour_line, neighbour_face) = lax.optimization_barrier(
        (own, residual, pivot_inverse, lower_blocks, upper_blocks, flux_jacobian, lift_operator,
         neighbour_line, neighbour_face)
    )
    up1 = z_shift(own, 1)
    down1 = z_shift(own, -1)
    lower_came = came_blocks(lower_blocks)
    upper_came = came_blocks(upper_blocks)
    lift = high_low(lift_operator.T)
    l_split, up_all = chip_chain(lower_blocks, lower_came, (3, 2, 1, 0))
    pivot = pivot_parts()
    asked = (neighbour_line * FACES + neighbour_face).reshape(1, SLOTS)
    table = jnp.concatenate([asked, y_shift(asked, -1)])
    up1, down1, l_split, up_all, upper_came, pivot, table, lift = lax.optimization_barrier(
        (up1, down1, l_split, up_all, upper_came, pivot, table, lift)
    )
    up2 = z_shift(up1, 1)
    down2 = z_shift(down1, -1)
    m1 = chip_shift(up_all, 1, (1, 2))
    m2 = chip_shift(up_all, 2, (1,))
    u_split, down_all = chip_chain(upper_blocks, upper_came, (0, 1, 2, 3))
    n1 = chip_shift(down_all, -1, (2, 1))
    n2 = chip_shift(down_all, -2, (2,))
    up2, down2, u_split, down_all = lax.optimization_barrier((up2, down2, u_split, down_all))
    up3 = z_shift(up2, 1)
    down3 = z_shift(down2, -1)
    table = jnp.concatenate([table, y_shift(table, 2)])
    up3, down3, table, m1 = lax.optimization_barrier((up3, down3, table, m1))
    up_half, down_half = call(
        halves_kernel, "halves", [VMEM] * 2, [f32(HALF, NF, ROW)] * 2, (up3, down3), 0, mib=4
    )
    up4 = z_shift(up_half, 1)
    down4 = z_shift(down_half, -1)
    up4, down4, m2 = lax.optimization_barrier((up4, down4, m2))

    def pick(name, parts, merges=(), relays=()):
        return call(
            pick_kernel(parts, merges), name, [SMEM] * 2 + [VMEM] * (9 + len(relays)),
            [f32(count, NF, ROW) for _, _, count in parts],
            (table, place, own, up1, up2, up3, down1, down2, down3, up4, down4, *relays),
            0, mib=12,
        )

    far_a, far_b, next_b, prev_a = pick(
        "pick_far", ((2, 0, HALF), (2, HALF, HALF), (1, HALF, HALF), (3, 0, HALF))
    )
    far_a = y_shift(far_a, 1)
    far_b = y_shift(far_b, -1)
    below_b = y_shift(next_b, 1)
    above_a = y_shift(prev_a, -1)
    far_a, far_b, n1 = lax.optimization_barrier((far_a, far_b, n1))
    next_a, prev_b = pick(
        "pick_near", ((1, 0, HALF), (3, HALF, HALF)), (YS - 1, 1), (far_a, far_b)
    )
    below_a = y_shift(next_a, 1)
    above_b = y_shift(prev_b, -1)
    (mine,) = pick("pick_own", ((0, 0, SLOTS),))
    below_a, above_b, n2 = lax.optimization_barrier((below_a, above_b, n2))

    matmul = 2 * NB * NB * ROW * 3
    kept, sent = call(
        driving_kernel, "driving", [SMEM] * 3 + [VMEM] * 5 + [VMEM] * 6,
        [f32(2, NB, ROW)] * 2,
        (table, place, core_ref, mine, below_a, below_b, above_a, above_b,
         flux_jacobian, *lift, *pivot),
        20 * matmul,
        [pltpu.VMEM((NB, ROW), jnp.float32), pltpu.VMEM((LINE_ROWS, NB, ROW), jnp.float32)],
    )
    driving, last = call(
        forward_kernel, "forward", [SMEM] * 2 + [VMEM] * 4, [f32(4, NB, ROW), f32(NB, ROW)],
        (core_ref, alive, kept, core_swap(sent), *l_split), 6 * matmul,
    )
    split_scratch = [pltpu.VMEM((2, NB, NB), jnp.bfloat16)] * 4
    sweep, first = call(
        middle_kernel, "middle", [SMEM] + [VMEM] * 10, [f32(4, NB, ROW), f32(NB, ROW)],
        (alive, chip_shift(last, 1), chip_shift(last, 2), chip_shift(last, 3),
         m1, m2, driving, *l_split, *u_split), 18 * matmul, split_scratch, mib=24,
    )
    kept, sent = call(
        backward_kernel, "backward", [SMEM] * 2 + [VMEM] * 8, [f32(2, 2, NV, NB)] * 2,
        (core_ref, alive, chip_shift(first, -1), chip_shift(first, -2), chip_shift(first, -3),
         n1, n2, sweep, *u_split), 12 * matmul,
        [pltpu.VMEM((NB, ROW), jnp.float32)] + split_scratch,
    )
    came = core_swap(sent)
    return jnp.where(
        core == 0,
        jnp.concatenate([kept, came], axis=0),
        jnp.concatenate([came, kept], axis=0),
    )


def solution(mesh):
    return jax.shard_map(
        local,
        mesh=mesh,
        in_specs=(
            P("span", "line", None, None),
            P("span", "line", None, None),
            P("span", "line", None, None),
            P("span", "line", None, None),
            P("span", "line", None, None),
            P("span", "line", None, None),
            P(),
            P(),
            P("span"),
            P("span", None),
            P("span", None),
        ),
        out_specs=P("span", "line", None, None),
        check_vma=False,
    )
```

```python
import jax
import jax.numpy as jnp
from jax import lax
from jax.experimental import pallas as pl
from jax.experimental.pallas import tpu as pltpu
from jax.sharding import PartitionSpec as P


NB = 320
NF = 80
FACES = 4
NV = 64
ROW = 128
YS, ZS = 4, 8
LINE_ROWS = 4
SLOTS = LINE_ROWS * FACES
HALF = SLOTS // 2


VMEM = pl.BlockSpec(memory_space=pltpu.VMEM)
SMEM = pl.BlockSpec(memory_space=pltpu.SMEM)


def f32(*shape):
    return jax.ShapeDtypeStruct(shape, jnp.float32)


def z_shift(array, by):
    pairs = [(y * ZS + z, y * ZS + (z + by) % ZS) for y in range(YS) for z in range(ZS)]
    return lax.ppermute(array, "span", pairs)


def y_shift(array, by):
    pairs = [(y * ZS + z, (y + by) % YS * ZS + z) for y in range(YS) for z in range(ZS)]
    return lax.ppermute(array, "span", pairs)


def y_shift_cross(array, by):
    spans = YS * ZS
    pairs = [
        (i * spans + y * ZS + z, (i ^ 1) * spans + (y + by) % YS * ZS + z)
        for i in range(8)
        for y in range(YS)
        for z in range(ZS)
    ]
    return lax.ppermute(array, ("line", "span"), pairs)


def core_swap(array):
    return lax.ppermute(array, "line", [(i, i ^ 1) for i in range(8)])


def chip_shift(array, by, chips=range(4)):
    pairs = [
        (2 * x + core, 2 * (x + by) + core)
        for x in chips
        for core in range(2)
        if 0 <= x + by < 4
    ]
    return lax.ppermute(array, "line", pairs)


def high_low(array):
    high = lax.reduce_precision(array, 8, 7)
    return high.astype(jnp.bfloat16), (array - high).astype(jnp.bfloat16)


def split_value(x):
    high = x.astype(jnp.bfloat16)
    return high, (x - high.astype(jnp.float32)).astype(jnp.bfloat16)


def product(w_high, w_low, x_high, x_both):
    wide = jnp.dot(w_high, x_both, preferred_element_type=jnp.float32)
    low = jnp.dot(w_low, x_high, preferred_element_type=jnp.float32)
    return wide[:, :ROW] + wide[:, ROW:] + low


def left_lanes():
    return lax.broadcasted_iota(jnp.int32, (NB, ROW), 1) < NV


def apply_pair(w_high, w_low, first, second, x):
    high, low = split_value(x)
    both = jnp.concatenate([high, low], axis=1)
    left = product(w_high[first], w_low[first], high, both)
    right = product(w_high[second], w_low[second], high, both)
    return jnp.where(left_lanes(), left, right)


def pick_kernel(parts):
    def kernel(table, place, own, up1, up2, up3, down1, down2, down3, up4, down4, *refs):
        y, z, core = place[0], place[1], place[2]
        whole = ((0, own), (7, up1), (6, up2), (5, up3), (1, down1), (2, down2), (3, down3))
        relays, outs = list(refs[: -len(parts)]), refs[-len(parts) :]
        for out, (dy, other, relayed) in zip(outs, parts):
            first = (1 - core if other else core) * HALF
            relay = relays.pop(0) if relayed else None

            def body(i, carry):
                asked = table[dy, first + i]
                owner, piece = asked // SLOTS, asked % SLOTS
                dz = (owner % ZS - z + ZS) % ZS

                @pl.when(owner // ZS == y)
                def _():
                    for k, source in whole:
                        @pl.when(dz == k)
                        def _():
                            out[i] = source[piece]

                    @pl.when((dz == 4) & (piece < HALF))
                    def _():
                        out[i] = up4[jnp.minimum(piece, HALF - 1)]

                    @pl.when((dz == 4) & (piece >= HALF))
                    def _():
                        out[i] = down4[jnp.maximum(piece - HALF, 0)]

                if relayed:
                    @pl.when(owner // ZS == (y + relayed) % YS)
                    def _():
                        out[i] = relay[i]

                return carry

            lax.fori_loop(0, HALF, body, 0)

    return kernel


def halves_kernel(up, down, up_half, down_half):
    up_half[...] = up[:HALF]
    down_half[...] = down[HALF:]


def whole_product(left, right_high, right_low):
    high, low = split_value(left)
    total = jnp.dot(high, right_high, preferred_element_type=jnp.float32)
    total += jnp.dot(low, right_high, preferred_element_type=jnp.float32)
    return total + jnp.dot(high, right_low, preferred_element_type=jnp.float32)


def own_kernel(core, kept, came, given_kept, given_came, high, low, own):
    first = core[0] == 0
    across = (((1,), (1,)), ((), ()))
    for half in range(2):
        blocks = (kept, came) if half == 0 else (came, kept)
        given = (given_kept, given_came) if half == 0 else (given_came, given_kept)
        values = []
        for element in range(2):
            block = jnp.where(first, blocks[0][0, element], blocks[1][0, element])
            w_high, w_low = split_value(block)
            high[0, 2 * half + element], low[0, 2 * half + element] = w_high, w_low
            x_high, x_low = split_value(jnp.where(first, given[0][0, element], given[1][0, element]))
            value = lax.dot_general(w_high, x_high, across, preferred_element_type=jnp.float32)
            value += lax.dot_general(w_high, x_low, across, preferred_element_type=jnp.float32)
            value += lax.dot_general(w_low, x_high, across, preferred_element_type=jnp.float32)
            values.append(value)
        own[0, half] = jnp.concatenate(values, axis=1)


def chain_kernel(order):
    def kernel(core, alive, kept, came, high, low, total):
        first = core[0] == 0
        for element in range(4):
            pair = (kept, came) if element < 2 else (came, kept)
            block = jnp.where(first, pair[0][0, element % 2], pair[1][0, element % 2])
            high[0, element], low[0, element] = split_value(block)
            if element == order[0]:
                start = block
        value = start
        for element in order[1:]:
            value = whole_product(value, high[0, element], low[0, element])
        total[0] = value * alive[pl.program_id(0), 3]

    return kernel


def alive_lanes(alive, element):
    lane = lax.broadcasted_iota(jnp.int32, (1, ROW), 1)
    return jnp.where(lane < NV, alive[0, element], alive[1, element])


def forward_kernel(table, place, alive, mine, below, above, mine_cross, below_cross, above_cross,
                   jacobian, jacobian_came, lift_high, lift_low, pivot_high, pivot_low, own,
                   l_high, l_low, out, last, held, terms):
    y, core = place[0], place[2]
    left = left_lanes()
    row = lax.broadcasted_iota(jnp.int32, (NB, NB), 0) // NF
    column = lax.broadcasted_iota(jnp.int32, (NB, NB), 1) // NF
    own_face = row == column

    def line_step(line, carry):
        for cross in range(2):
            half = 1 - core if cross else core
            here, down, up = (mine_cross, below_cross, above_cross) if cross else (mine, below, above)
            source = jacobian_came if cross else jacobian
            for face in range(FACES):
                slot = line * FACES + face
                dy = (table[0, core * HALF + slot] // (SLOTS * ZS) - y + YS) % YS
                from_below = (dy == 3) if cross else (dy >= 2)
                value = jnp.where(from_below, down[slot], up[slot])
                held[pl.ds(face * NF, NF), :] = jnp.where(dy == 0, here[slot], value)
            high, low = split_value(held[...])
            both = jnp.concatenate([high, low], axis=1)
            fluxes = []
            for element in range(2):
                tiled = jnp.concatenate([source[core * 2 + line, element]] * FACES, axis=0)
                wide = split_value(jnp.where(own_face, tiled, 0.0))
                fluxes.append(product(*wide, high, both))
            high, low = split_value(jnp.where(left, *fluxes))
            both = jnp.concatenate([high, low], axis=1)
            term = product(lift_high[...], lift_low[...], high, both)
            first = 4 * line + 2 * half
            term = apply_pair(pivot_high, pivot_low, first, first + 1, term)
            terms[line, half] = own[line, half] - term
        return carry

    lax.fori_loop(0, 2, line_step, 0)
    for half in range(2):
        first, second = terms[0, half], terms[1, half]
        out[2 * half] = jnp.where(left, first, pltpu.roll(second, NV, 1))
        out[2 * half + 1] = jnp.where(left, pltpu.roll(first, NV, 1), second)
    last[...] = out[0] * alive_lanes(alive, 0)

    def step(element, carry):
        term = apply_pair(l_high, l_low, element, 4 + element, last[...])
        last[...] = (out[element] + term) * alive_lanes(alive, element)
        return carry

    lax.fori_loop(1, 4, step, 0)


def enter(near, mid, far, close, apart):
    value = mid[...] + apply_pair(*apart, 0, 1, far[...])
    return near[...] + apply_pair(*close, 0, 1, value)


def split_blocks(source, high, low):
    for line in range(2):
        high[line], low[line] = split_value(source[line])


def middle_kernel(alive, near, mid, far, close, apart, driving,
                  l_high, l_low, u_high, u_low, sweep, first, *split):
    split_blocks(close, *split[:2])
    split_blocks(apart, *split[2:])
    first[...] = enter(near, mid, far, split[:2], split[2:])

    def up(element, carry):
        term = apply_pair(l_high, l_low, element, 4 + element, first[...])
        first[...] = (driving[element] + term) * alive_lanes(alive, element)
        sweep[element] = first[...]
        return carry

    lax.fori_loop(0, 4, up, 0)

    def down(step, carry):
        element = 2 - step
        term = apply_pair(u_high, u_low, element, 4 + element, first[...])
        first[...] = (sweep[element] + term) * alive_lanes(alive, element)
        return carry

    lax.fori_loop(0, 3, down, 0)


def backward_kernel(core, alive, near, mid, far, close, apart, sweep,
                    u_high, u_low, kept, sent, held, *split):
    split_blocks(close, *split[:2])
    split_blocks(apart, *split[2:])
    held[...] = enter(near, mid, far, split[:2], split[2:])

    def down(step, carry):
        element = 3 - step
        term = apply_pair(u_high, u_low, element, 4 + element, held[...])
        value = (sweep[element] + term) * alive_lanes(alive, element)
        held[...] = value
        natural = jnp.transpose(value)

        @pl.when(element // 2 == core[0])
        def _():
            kept[0, element % 2] = natural[:NV]
            kept[1, element % 2] = natural[NV:]

        @pl.when(element // 2 != core[0])
        def _():
            sent[0, element % 2] = natural[:NV]
            sent[1, element % 2] = natural[NV:]

        return carry

    lax.fori_loop(0, 4, down, 0)


def call(kernel, specs, out_shape, operands, flops, scratch=(), mib=16):
    out_specs = jax.tree.map(lambda _: VMEM, out_shape)
    moved = sum(4 * o.size for o in jax.tree.leaves((operands, out_shape)))
    return pl.pallas_call(
        kernel,
        out_shape=out_shape,
        in_specs=specs,
        out_specs=out_specs,
        scratch_shapes=list(scratch),
        compiler_params=pltpu.CompilerParams(vmem_limit_bytes=mib << 20),
        cost_estimate=pl.CostEstimate(flops=flops, bytes_accessed=moved, transcendentals=0),
    )(*operands)


def local(
    residual,
    previous,
    pivot_inverse,
    lower_blocks,
    upper_blocks,
    flux_jacobian,
    trace_operator,
    lift_operator,
    lengths,
    neighbour_line,
    neighbour_face,
):
    high = lax.Precision.HIGH
    line_pos = lax.axis_index("line")
    span_pos = lax.axis_index("span")
    core = line_pos % 2
    elements = residual.shape[1]
    position = line_pos * elements + jnp.arange(elements, dtype=jnp.int32)
    live = (position[None, :] < lengths[:, None]).astype(jnp.float32)
    place = jnp.stack([span_pos // ZS, span_pos % ZS, core]).astype(jnp.int32)
    core_ref = core.astype(jnp.int32).reshape(1)

    masked = (previous * live[:, :, None, None]).reshape(LINE_ROWS, ROW, NB)
    own = jnp.einsum("lmn,nk->lkm", masked, trace_operator, precision=high)
    own = own.reshape(SLOTS, NF, ROW)

    chip_position = line_pos // 2 * 4 + jnp.arange(4, dtype=jnp.int32)
    chip_lengths = lax.dynamic_slice_in_dim(lengths, core * 2, 2, 0)
    alive = (chip_position[None, :] < chip_lengths[:, None]).astype(jnp.float32)
    block = (1, 2, NB, NB)

    def chip_chain(blocks, came, order):
        split_shape = jax.ShapeDtypeStruct((2, 4, NB, NB), jnp.bfloat16)
        split_spec = pl.BlockSpec((1, 4, NB, NB), lambda i, core, alive: (i, 0, 0, 0))
        split_high, split_low, total = pl.pallas_call(
            chain_kernel(order),
            name="chain",
            grid_spec=pltpu.PrefetchScalarGridSpec(
                num_scalar_prefetch=2,
                grid=(2,),
                in_specs=[
                    pl.BlockSpec(block, lambda i, core, alive: (core[0] * 2 + i, 0, 0, 0)),
                    pl.BlockSpec(block, lambda i, core, alive: (core[0] * 2 + i, 0, 0, 0)),
                ],
                out_specs=[
                    split_spec,
                    split_spec,
                    pl.BlockSpec((1, NB, NB), lambda i, core, alive: (i, 0, 0)),
                ],
            ),
            out_shape=[split_shape, split_shape, f32(2, NB, NB)],
            compiler_params=pltpu.CompilerParams(vmem_limit_bytes=60 << 20),
            cost_estimate=pl.CostEstimate(
                flops=36 * NB**3, bytes_accessed=32 * NB * NB, transcendentals=0
            ),
        )(core_ref, alive, blocks, came)
        return (split_high.reshape(8, NB, NB), split_low.reshape(8, NB, NB)), total

    def pivot_parts(came, given_came):
        split_shape = jax.ShapeDtypeStruct((2, 4, NB, NB), jnp.bfloat16)
        split_spec = pl.BlockSpec((1, 4, NB, NB), lambda i, core: (i, 0, 0, 0))
        spec = pl.BlockSpec(block, lambda i, core: (core[0] * 2 + i, 0, 0, 0))
        given = pl.BlockSpec((1, 2, NV, NB), lambda i, core: (core[0] * 2 + i, 0, 0, 0))
        high, low, own = pl.pallas_call(
            own_kernel,
            name="own",
            grid_spec=pltpu.PrefetchScalarGridSpec(
                num_scalar_prefetch=1,
                grid=(2,),
                in_specs=[spec, spec, given, given],
                out_specs=[
                    split_spec,
                    split_spec,
                    pl.BlockSpec((1, 2, NB, ROW), lambda i, core: (i, 0, 0, 0)),
                ],
            ),
            out_shape=[split_shape, split_shape, f32(2, 2, NB, ROW)],
            compiler_params=pltpu.CompilerParams(vmem_limit_bytes=60 << 20),
            cost_estimate=pl.CostEstimate(
                flops=48 * NB * NB * NV, bytes_accessed=64 * NB * NB, transcendentals=0
            ),
        )(core_ref, pivot_inverse, came, residual, given_came)
        return high.reshape(8, NB, NB), low.reshape(8, NB, NB), own

    (own, residual, pivot_inverse, lower_blocks, upper_blocks, flux_jacobian, lift_operator,
     neighbour_line, neighbour_face) = lax.optimization_barrier(
        (own, residual, pivot_inverse, lower_blocks, upper_blocks, flux_jacobian, lift_operator,
         neighbour_line, neighbour_face)
    )
    up1 = z_shift(own, 1)
    down1 = z_shift(own, -1)
    lower_came = core_swap(lower_blocks)
    upper_came = core_swap(upper_blocks)
    lift = high_low(lift_operator.T)
    l_split, up_all = chip_chain(lower_blocks, lower_came, (3, 2, 1, 0))
    asked = (neighbour_line * FACES + neighbour_face).reshape(1, SLOTS)
    table = jnp.concatenate([asked, y_shift(asked, -1)])
    up1, down1, l_split, up_all, upper_came, table, lift = lax.optimization_barrier(
        (up1, down1, l_split, up_all, upper_came, table, lift)
    )
    up2 = z_shift(up1, 1)
    down2 = z_shift(down1, -1)
    m1 = chip_shift(up_all, 1, (1, 2))
    m2 = chip_shift(up_all, 2, (1,))
    pivot_came = core_swap(pivot_inverse)
    residual_came = core_swap(residual)
    jacobian_came = core_swap(flux_jacobian)
    u_split, down_all = chip_chain(upper_blocks, upper_came, (0, 1, 2, 3))
    n1 = chip_shift(down_all, -1, (2, 1))
    n2 = chip_shift(down_all, -2, (2,))
    up2, down2, u_split, down_all, pivot_came, residual_came, jacobian_came = (
        lax.optimization_barrier(
            (up2, down2, u_split, down_all, pivot_came, residual_came, jacobian_came)
        )
    )
    up3 = z_shift(up2, 1)
    down3 = z_shift(down2, -1)
    pivot = pivot_parts(pivot_came, residual_came)
    table = jnp.concatenate([table, y_shift(table, 2)])
    up3, down3, table, pivot = lax.optimization_barrier((up3, down3, table, pivot))
    up_half, down_half = call(
        halves_kernel, [VMEM] * 2, [f32(HALF, NF, ROW)] * 2, (up3, down3), 0, mib=4
    )
    up4 = z_shift(up_half, 1)
    down4 = z_shift(down_half, -1)

    def pick(parts, relays=()):
        return call(
            pick_kernel(parts), [SMEM] * 2 + [VMEM] * (9 + len(relays)),
            [f32(HALF, NF, ROW)] * len(parts),
            (table, place, own, up1, up2, up3, down1, down2, down3, up4, down4, *relays),
            0, mib=12,
        )

    far, far_other, next_other, prev_own = pick(
        ((2, False, 0), (2, True, 0), (1, True, 0), (3, False, 0))
    )
    far = y_shift(far, 1)
    far_other = y_shift(far_other, -1)
    below_cross = y_shift_cross(next_other, 1)
    above = y_shift(prev_own, -1)
    next_own, prev_other = pick(((1, False, YS - 1), (3, True, 1)), (far, far_other))
    below = y_shift(next_own, 1)
    above_cross = y_shift_cross(prev_other, -1)
    mine, mine_other = pick(((0, False, 0), (0, True, 0)))
    mine_cross = core_swap(mine_other)

    matmul = 2 * NB * NB * ROW * 3
    driving, last = call(
        forward_kernel, [SMEM] * 3 + [VMEM] * 15, [f32(4, NB, ROW), f32(NB, ROW)],
        (table, place, alive, mine, below, above, mine_cross, below_cross, above_cross,
         flux_jacobian, jacobian_came, *lift, *pivot, *l_split),
        26 * matmul,
        [pltpu.VMEM((NB, ROW), jnp.float32), pltpu.VMEM((2, 2, NB, ROW), jnp.float32)],
        mib=24,
    )
    driving, last, m1, m2, n1, n2 = lax.optimization_barrier((driving, last, m1, m2, n1, n2))
    split_scratch = [pltpu.VMEM((2, NB, NB), jnp.bfloat16)] * 4
    sweep, first = call(
        middle_kernel, [SMEM] + [VMEM] * 10, [f32(4, NB, ROW), f32(NB, ROW)],
        (alive, chip_shift(last, 1), chip_shift(last, 2), chip_shift(last, 3),
         m1, m2, driving, *l_split, *u_split), 18 * matmul, split_scratch, mib=24,
    )
    kept, sent = call(
        backward_kernel, [SMEM] * 2 + [VMEM] * 8, [f32(2, 2, NV, NB)] * 2,
        (core_ref, alive, chip_shift(first, -1), chip_shift(first, -2), chip_shift(first, -3),
         n1, n2, sweep, *u_split), 12 * matmul,
        [pltpu.VMEM((NB, ROW), jnp.float32)] + split_scratch,
    )
    came = core_swap(sent)
    return jnp.where(
        core == 0,
        jnp.concatenate([kept, came], axis=0),
        jnp.concatenate([came, kept], axis=0),
    )


def solution(mesh):
    return jax.shard_map(
        local,
        mesh=mesh,
        in_specs=(
            P("span", "line", None, None),
            P("span", "line", None, None),
            P("span", "line", None, None),
            P("span", "line", None, None),
            P("span", "line", None, None),
            P("span", "line", None, None),
            P(),
            P(),
            P("span"),
            P("span", None),
            P("span", None),
        ),
        out_specs=P("span", "line", None, None),
        check_vma=False,
    )
```

```python
import jax
import jax.numpy as jnp
from jax import lax
from jax.experimental import pallas as pl
from jax.experimental.pallas import tpu as pltpu
from jax.sharding import PartitionSpec as P


NB = 320
NF = 80
FACES = 4
NV = 64
ROW = 128
YS, ZS = 4, 8
LINE_ROWS = 4
SLOTS = LINE_ROWS * FACES
HALF = SLOTS // 2


VMEM = pl.BlockSpec(memory_space=pltpu.VMEM)
SMEM = pl.BlockSpec(memory_space=pltpu.SMEM)


def f32(*shape):
    return jax.ShapeDtypeStruct(shape, jnp.float32)


def z_shift(array, by):
    pairs = [(y * ZS + z, y * ZS + (z + by) % ZS) for y in range(YS) for z in range(ZS)]
    return lax.ppermute(array, "span", pairs)


def y_shift(array, by):
    pairs = [(y * ZS + z, (y + by) % YS * ZS + z) for y in range(YS) for z in range(ZS)]
    return lax.ppermute(array, "span", pairs)


def y_shift_cross(array, by):
    spans = YS * ZS
    pairs = [
        (i * spans + y * ZS + z, (i ^ 1) * spans + (y + by) % YS * ZS + z)
        for i in range(8)
        for y in range(YS)
        for z in range(ZS)
    ]
    return lax.ppermute(array, ("line", "span"), pairs)


def core_swap(array):
    return lax.ppermute(array, "line", [(i, i ^ 1) for i in range(8)])


def chip_shift(array, by, chips=range(4)):
    pairs = [
        (2 * x + core, 2 * (x + by) + core)
        for x in chips
        for core in range(2)
        if 0 <= x + by < 4
    ]
    return lax.ppermute(array, "line", pairs)


def high_low(array):
    high = lax.reduce_precision(array, 8, 7)
    return high.astype(jnp.bfloat16), (array - high).astype(jnp.bfloat16)


def split_value(x):
    high = x.astype(jnp.bfloat16)
    return high, (x - high.astype(jnp.float32)).astype(jnp.bfloat16)


def product(w_high, w_low, x_high, x_both):
    wide = jnp.dot(w_high, x_both, preferred_element_type=jnp.float32)
    low = jnp.dot(w_low, x_high, preferred_element_type=jnp.float32)
    return wide[:, :ROW] + wide[:, ROW:] + low


def left_lanes():
    return lax.broadcasted_iota(jnp.int32, (NB, ROW), 1) < NV


def apply_pair(w_high, w_low, first, second, x):
    high, low = split_value(x)
    both = jnp.concatenate([high, low], axis=1)
    left = product(w_high[first], w_low[first], high, both)
    right = product(w_high[second], w_low[second], high, both)
    return jnp.where(left_lanes(), left, right)


def pick_kernel(parts):
    def kernel(table, place, own, up1, up2, up3, down1, down2, down3, up4, down4, *refs):
        y, z, core = place[0], place[1], place[2]
        whole = ((0, own), (7, up1), (6, up2), (5, up3), (1, down1), (2, down2), (3, down3))
        relays, outs = list(refs[: -len(parts)]), refs[-len(parts) :]
        for out, (dy, other, relayed) in zip(outs, parts):
            first = (1 - core if other else core) * HALF
            relay = relays.pop(0) if relayed else None

            def body(i, carry):
                asked = table[dy, first + i]
                owner, piece = asked // SLOTS, asked % SLOTS
                dz = (owner % ZS - z + ZS) % ZS

                @pl.when(owner // ZS == y)
                def _():
                    for k, source in whole:
                        @pl.when(dz == k)
                        def _():
                            out[i] = source[piece]

                    @pl.when((dz == 4) & (piece < HALF))
                    def _():
                        out[i] = up4[jnp.minimum(piece, HALF - 1)]

                    @pl.when((dz == 4) & (piece >= HALF))
                    def _():
                        out[i] = down4[jnp.maximum(piece - HALF, 0)]

                if relayed:
                    @pl.when(owner // ZS == (y + relayed) % YS)
                    def _():
                        out[i] = relay[i]

                return carry

            lax.fori_loop(0, HALF, body, 0)

    return kernel


def halves_kernel(up, down, up_half, down_half):
    up_half[...] = up[:HALF]
    down_half[...] = down[HALF:]


def whole_product(left, right_high, right_low):
    high, low = split_value(left)
    total = jnp.dot(high, right_high, preferred_element_type=jnp.float32)
    total += jnp.dot(low, right_high, preferred_element_type=jnp.float32)
    return total + jnp.dot(high, right_low, preferred_element_type=jnp.float32)


def own_kernel(core, kept, came, given_kept, given_came, high, low, own):
    first = core[0] == 0
    across = (((1,), (1,)), ((), ()))
    for half in range(2):
        blocks = (kept, came) if half == 0 else (came, kept)
        given = (given_kept, given_came) if half == 0 else (given_came, given_kept)
        values = []
        for element in range(2):
            block = jnp.where(first, blocks[0][0, element], blocks[1][0, element])
            w_high, w_low = split_value(block)
            high[0, 2 * half + element], low[0, 2 * half + element] = w_high, w_low
            x_high, x_low = split_value(jnp.where(first, given[0][0, element], given[1][0, element]))
            value = lax.dot_general(w_high, x_high, across, preferred_element_type=jnp.float32)
            value += lax.dot_general(w_high, x_low, across, preferred_element_type=jnp.float32)
            value += lax.dot_general(w_low, x_high, across, preferred_element_type=jnp.float32)
            values.append(value)
        own[0, half] = jnp.concatenate(values, axis=1)


def chain_kernel(order):
    def kernel(core, alive, kept, came, high, low, total):
        first = core[0] == 0
        for element in range(4):
            pair = (kept, came) if element < 2 else (came, kept)
            block = jnp.where(first, pair[0][0, element % 2], pair[1][0, element % 2])
            high[0, element], low[0, element] = split_value(block)
            if element == order[0]:
                start = block
        value = start
        for element in order[1:]:
            value = whole_product(value, high[0, element], low[0, element])
        total[0] = value * alive[pl.program_id(0), 3]

    return kernel


def alive_lanes(alive, element):
    lane = lax.broadcasted_iota(jnp.int32, (1, ROW), 1)
    return jnp.where(lane < NV, alive[0, element], alive[1, element])


def forward_kernel(table, place, alive, mine, below, above, mine_cross, below_cross, above_cross,
                   jacobian, jacobian_came, lift_high, lift_low, pivot_high, pivot_low, own,
                   l_high, l_low, out, last, held, terms):
    y, core = place[0], place[2]
    left = left_lanes()
    row = lax.broadcasted_iota(jnp.int32, (NB, NB), 0) // NF
    column = lax.broadcasted_iota(jnp.int32, (NB, NB), 1) // NF
    own_face = row == column

    def line_step(line, carry):
        for cross in range(2):
            half = 1 - core if cross else core
            here, down, up = (mine_cross, below_cross, above_cross) if cross else (mine, below, above)
            source = jacobian_came if cross else jacobian
            for face in range(FACES):
                slot = line * FACES + face
                dy = (table[0, core * HALF + slot] // (SLOTS * ZS) - y + YS) % YS
                from_below = (dy == 3) if cross else (dy >= 2)
                value = jnp.where(from_below, down[slot], up[slot])
                held[pl.ds(face * NF, NF), :] = jnp.where(dy == 0, here[slot], value)
            high, low = split_value(held[...])
            both = jnp.concatenate([high, low], axis=1)
            fluxes = []
            for element in range(2):
                tiled = jnp.concatenate([source[core * 2 + line, element]] * FACES, axis=0)
                wide = split_value(jnp.where(own_face, tiled, 0.0))
                fluxes.append(product(*wide, high, both))
            high, low = split_value(jnp.where(left, *fluxes))
            both = jnp.concatenate([high, low], axis=1)
            term = product(lift_high[...], lift_low[...], high, both)
            first = 4 * line + 2 * half
            term = apply_pair(pivot_high, pivot_low, first, first + 1, term)
            terms[line, half] = own[line, half] - term
        return carry

    lax.fori_loop(0, 2, line_step, 0)
    for half in range(2):
        first, second = terms[0, half], terms[1, half]
        out[2 * half] = jnp.where(left, first, pltpu.roll(second, NV, 1))
        out[2 * half + 1] = jnp.where(left, pltpu.roll(first, NV, 1), second)
    last[...] = out[0] * alive_lanes(alive, 0)

    def step(element, carry):
        term = apply_pair(l_high, l_low, element, 4 + element, last[...])
        last[...] = (out[element] + term) * alive_lanes(alive, element)
        return carry

    lax.fori_loop(1, 4, step, 0)


def enter(near, mid, far, close, apart):
    value = mid[...] + apply_pair(*apart, 0, 1, far[...])
    return near[...] + apply_pair(*close, 0, 1, value)


def split_blocks(source, high, low):
    for line in range(2):
        high[line], low[line] = split_value(source[line])


def middle_kernel(alive, near, mid, far, close, apart, driving,
                  l_high, l_low, u_high, u_low, sweep, first, *split):
    split_blocks(close, *split[:2])
    split_blocks(apart, *split[2:])
    first[...] = enter(near, mid, far, split[:2], split[2:])

    def up(element, carry):
        term = apply_pair(l_high, l_low, element, 4 + element, first[...])
        first[...] = (driving[element] + term) * alive_lanes(alive, element)
        sweep[element] = first[...]
        return carry

    lax.fori_loop(0, 4, up, 0)

    def down(step, carry):
        element = 2 - step
        term = apply_pair(u_high, u_low, element, 4 + element, first[...])
        first[...] = (sweep[element] + term) * alive_lanes(alive, element)
        return carry

    lax.fori_loop(0, 3, down, 0)


def backward_kernel(core, alive, near, mid, far, close, apart, sweep,
                    u_high, u_low, kept, sent, held, *split):
    split_blocks(close, *split[:2])
    split_blocks(apart, *split[2:])
    held[...] = enter(near, mid, far, split[:2], split[2:])

    def down(step, carry):
        element = 3 - step
        term = apply_pair(u_high, u_low, element, 4 + element, held[...])
        value = (sweep[element] + term) * alive_lanes(alive, element)
        held[...] = value
        natural = jnp.transpose(value)

        @pl.when(element // 2 == core[0])
        def _():
            kept[0, element % 2] = natural[:NV]
            kept[1, element % 2] = natural[NV:]

        @pl.when(element // 2 != core[0])
        def _():
            sent[0, element % 2] = natural[:NV]
            sent[1, element % 2] = natural[NV:]

        return carry

    lax.fori_loop(0, 4, down, 0)


def call(kernel, specs, out_shape, operands, flops, scratch=(), mib=16):
    out_specs = jax.tree.map(lambda _: VMEM, out_shape)
    moved = sum(4 * o.size for o in jax.tree.leaves((operands, out_shape)))
    return pl.pallas_call(
        kernel,
        out_shape=out_shape,
        in_specs=specs,
        out_specs=out_specs,
        scratch_shapes=list(scratch),
        compiler_params=pltpu.CompilerParams(vmem_limit_bytes=mib << 20),
        cost_estimate=pl.CostEstimate(flops=flops, bytes_accessed=moved, transcendentals=0),
    )(*operands)


def local(
    residual,
    previous,
    pivot_inverse,
    lower_blocks,
    upper_blocks,
    flux_jacobian,
    trace_operator,
    lift_operator,
    lengths,
    neighbour_line,
    neighbour_face,
):
    high = lax.Precision.HIGH
    line_pos = lax.axis_index("line")
    span_pos = lax.axis_index("span")
    core = line_pos % 2
    elements = residual.shape[1]
    position = line_pos * elements + jnp.arange(elements, dtype=jnp.int32)
    live = (position[None, :] < lengths[:, None]).astype(jnp.float32)
    place = jnp.stack([span_pos // ZS, span_pos % ZS, core]).astype(jnp.int32)
    core_ref = core.astype(jnp.int32).reshape(1)

    masked = (previous * live[:, :, None, None]).reshape(LINE_ROWS, ROW, NB)
    own = jnp.einsum("lmn,nk->lkm", masked, trace_operator, precision=high)
    own = own.reshape(SLOTS, NF, ROW)

    chip_position = line_pos // 2 * 4 + jnp.arange(4, dtype=jnp.int32)
    chip_lengths = lax.dynamic_slice_in_dim(lengths, core * 2, 2, 0)
    alive = (chip_position[None, :] < chip_lengths[:, None]).astype(jnp.float32)
    block = (1, 2, NB, NB)

    def chip_chain(blocks, came, order):
        split_shape = jax.ShapeDtypeStruct((2, 4, NB, NB), jnp.bfloat16)
        split_spec = pl.BlockSpec((1, 4, NB, NB), lambda i, core, alive: (i, 0, 0, 0))
        split_high, split_low, total = pl.pallas_call(
            chain_kernel(order),
            name="chain",
            grid_spec=pltpu.PrefetchScalarGridSpec(
                num_scalar_prefetch=2,
                grid=(2,),
                in_specs=[
                    pl.BlockSpec(block, lambda i, core, alive: (core[0] * 2 + i, 0, 0, 0)),
                    pl.BlockSpec(block, lambda i, core, alive: (core[0] * 2 + i, 0, 0, 0)),
                ],
                out_specs=[
                    split_spec,
                    split_spec,
                    pl.BlockSpec((1, NB, NB), lambda i, core, alive: (i, 0, 0)),
                ],
            ),
            out_shape=[split_shape, split_shape, f32(2, NB, NB)],
            compiler_params=pltpu.CompilerParams(vmem_limit_bytes=60 << 20),
            cost_estimate=pl.CostEstimate(
                flops=36 * NB**3, bytes_accessed=32 * NB * NB, transcendentals=0
            ),
        )(core_ref, alive, blocks, came)
        return (split_high.reshape(8, NB, NB), split_low.reshape(8, NB, NB)), total

    def pivot_parts(came, given_came):
        split_shape = jax.ShapeDtypeStruct((2, 4, NB, NB), jnp.bfloat16)
        split_spec = pl.BlockSpec((1, 4, NB, NB), lambda i, core: (i, 0, 0, 0))
        spec = pl.BlockSpec(block, lambda i, core: (core[0] * 2 + i, 0, 0, 0))
        given = pl.BlockSpec((1, 2, NV, NB), lambda i, core: (core[0] * 2 + i, 0, 0, 0))
        high, low, own = pl.pallas_call(
            own_kernel,
            name="own",
            grid_spec=pltpu.PrefetchScalarGridSpec(
                num_scalar_prefetch=1,
                grid=(2,),
                in_specs=[spec, spec, given, given],
                out_specs=[
                    split_spec,
                    split_spec,
                    pl.BlockSpec((1, 2, NB, ROW), lambda i, core: (i, 0, 0, 0)),
                ],
            ),
            out_shape=[split_shape, split_shape, f32(2, 2, NB, ROW)],
            compiler_params=pltpu.CompilerParams(vmem_limit_bytes=20 << 20),
            cost_estimate=pl.CostEstimate(
                flops=48 * NB * NB * NV, bytes_accessed=64 * NB * NB, transcendentals=0
            ),
        )(core_ref, pivot_inverse, came, residual, given_came)
        return high.reshape(8, NB, NB), low.reshape(8, NB, NB), own

    (own, residual, pivot_inverse, lower_blocks, upper_blocks, flux_jacobian, lift_operator,
     neighbour_line, neighbour_face) = lax.optimization_barrier(
        (own, residual, pivot_inverse, lower_blocks, upper_blocks, flux_jacobian, lift_operator,
         neighbour_line, neighbour_face)
    )
    up1 = z_shift(own, 1)
    down1 = z_shift(own, -1)
    lower_came = core_swap(lower_blocks)
    upper_came = core_swap(upper_blocks)
    lift = high_low(lift_operator.T)
    asked = (neighbour_line * FACES + neighbour_face).reshape(1, SLOTS)
    table = jnp.concatenate([asked, y_shift(asked, -1)])
    up1, down1, lower_came, table, lift = lax.optimization_barrier(
        (up1, down1, lower_came, table, lift)
    )
    up2 = z_shift(up1, 1)
    down2 = z_shift(down1, -1)
    l_split, up_all = chip_chain(lower_blocks, lower_came, (3, 2, 1, 0))
    m1 = chip_shift(up_all, 1, (1, 2))
    m2 = chip_shift(up_all, 2, (1,))
    pivot_came = core_swap(pivot_inverse)
    residual_came = core_swap(residual)
    jacobian_came = core_swap(flux_jacobian)
    up2, down2, l_split, up_all, upper_came, pivot_came, residual_came, jacobian_came = (
        lax.optimization_barrier(
            (up2, down2, l_split, up_all, upper_came, pivot_came, residual_came, jacobian_came)
        )
    )
    up3 = z_shift(up2, 1)
    down3 = z_shift(down2, -1)
    u_split, down_all = chip_chain(upper_blocks, upper_came, (0, 1, 2, 3))
    n1 = chip_shift(down_all, -1, (2, 1))
    n2 = chip_shift(down_all, -2, (2,))
    table = jnp.concatenate([table, y_shift(table, 2)])
    up3, down3, table, u_split, down_all = lax.optimization_barrier(
        (up3, down3, table, u_split, down_all)
    )
    up_half, down_half = call(
        halves_kernel, [VMEM] * 2, [f32(HALF, NF, ROW)] * 2, (up3, down3), 0, mib=4
    )
    up4 = z_shift(up_half, 1)
    down4 = z_shift(down_half, -1)

    def pick(parts, relays=()):
        return call(
            pick_kernel(parts), [SMEM] * 2 + [VMEM] * (9 + len(relays)),
            [f32(HALF, NF, ROW)] * len(parts),
            (table, place, own, up1, up2, up3, down1, down2, down3, up4, down4, *relays),
            0, mib=12,
        )

    far, far_other, next_other, prev_own = pick(
        ((2, False, 0), (2, True, 0), (1, True, 0), (3, False, 0))
    )
    far = y_shift(far, 1)
    far_other = y_shift(far_other, -1)
    below_cross = y_shift_cross(next_other, 1)
    above = y_shift(prev_own, -1)
    next_own, prev_other = pick(((1, False, YS - 1), (3, True, 1)), (far, far_other))
    below = y_shift(next_own, 1)
    above_cross = y_shift_cross(prev_other, -1)
    pivot_came, next_own = lax.optimization_barrier((pivot_came, next_own))
    pivot = pivot_parts(pivot_came, residual_came)
    mine, mine_other = pick(((0, False, 0), (0, True, 0)))
    mine_cross = core_swap(mine_other)

    matmul = 2 * NB * NB * ROW * 3
    driving, last = call(
        forward_kernel, [SMEM] * 3 + [VMEM] * 15, [f32(4, NB, ROW), f32(NB, ROW)],
        (table, place, alive, mine, below, above, mine_cross, below_cross, above_cross,
         flux_jacobian, jacobian_came, *lift, *pivot, *l_split),
        26 * matmul,
        [pltpu.VMEM((NB, ROW), jnp.float32), pltpu.VMEM((2, 2, NB, ROW), jnp.float32)],
        mib=24,
    )
    driving, last, m1, m2 = lax.optimization_barrier((driving, last, m1, m2))
    split_scratch = [pltpu.VMEM((2, NB, NB), jnp.bfloat16)] * 4
    sweep, first = call(
        middle_kernel, [SMEM] + [VMEM] * 10, [f32(4, NB, ROW), f32(NB, ROW)],
        (alive, chip_shift(last, 1), chip_shift(last, 2), chip_shift(last, 3),
         m1, m2, driving, *l_split, *u_split), 18 * matmul, split_scratch, mib=24,
    )
    sweep, first, n1, n2 = lax.optimization_barrier((sweep, first, n1, n2))
    kept, sent = call(
        backward_kernel, [SMEM] * 2 + [VMEM] * 8, [f32(2, 2, NV, NB)] * 2,
        (core_ref, alive, chip_shift(first, -1), chip_shift(first, -2), chip_shift(first, -3),
         n1, n2, sweep, *u_split), 12 * matmul,
        [pltpu.VMEM((NB, ROW), jnp.float32)] + split_scratch,
    )
    came = core_swap(sent)
    return jnp.where(
        core == 0,
        jnp.concatenate([kept, came], axis=0),
        jnp.concatenate([came, kept], axis=0),
    )


def solution(mesh):
    return jax.shard_map(
        local,
        mesh=mesh,
        in_specs=(
            P("span", "line", None, None),
            P("span", "line", None, None),
            P("span", "line", None, None),
            P("span", "line", None, None),
            P("span", "line", None, None),
            P("span", "line", None, None),
            P(),
            P(),
            P("span"),
            P("span", None),
            P("span", None),
        ),
        out_specs=P("span", "line", None, None),
        check_vma=False,
    )
```
